256 devices in a mesh: tm: 8 (over y, core), rows: 32 (over z, x).
Axes of the slice: x: 4, y: 4, z: 8, core: 2. Of those that a mesh axis runs over, the one named last changes fastest.
Arguments:
- features: bfloat16 [32, 64, 320, 128], P('tm', 'rows'), may hold values from -20 to 20
- gain_one: float32 [128], replicated, may hold values from 0.1 to 1.9
- shift_one: float32 [128], replicated, may hold values from -4 to 4
- weight_one: bfloat16 [3456, 128], replicated, may hold values from -0.109375 to 0.109375
- bias_one: float32 [128], replicated, may hold values from -6 to 6
- gain_two: float32 [128], replicated, may hold values from 0.1 to 1.9
- shift_two: float32 [128], replicated, may hold values from -4 to 4
- weight_two: bfloat16 [3456, 128], replicated, may hold values from -0.109375 to 0.109375
- bias_two: float32 [128], replicated, may hold values from -6 to 6
Outputs:
- block_out: bfloat16 [32, 64, 320, 128], P('tm', 'rows')
The draws below stay inside these ranges and needn't reach their ends.
All inputs are finite; a program needn't handle non-finite values.
Results may differ from the reference program's by a relative error of at most 0.007.
Values may be sent and summed in bfloat16 or wider, within the bound.
No kernel may reach another device: no remote copies, remote signals or barrier semaphores. Data moves between devices by JAX's collectives and lax.ppermute only.
A program may use at most 64 MiB of HBM per device.

```python
import jax
import jax.numpy as jnp
from jax import lax

C = 128
GROUPS = 32
W = 320
NT = 32
H = 64


def draw_features(key, part):
    base_key = jax.random.fold_in(key, 17)
    noise_key, mean_key = jax.random.split(base_key, 2)
    frame_pos = jnp.arange(NT, dtype=jnp.float32) / max(NT - 1, 1)
    row_pos = jnp.arange(H, dtype=jnp.float32) / max(H - 1, 1)
    rising = 0.6 * (1.0 + frame_pos[:, None] + row_pos[None, :])
    offsets = jax.random.uniform(mean_key, (C,), jnp.float32, -0.6, 0.6)
    noise = jnp.clip(jax.random.normal(noise_key, (NT, H, W, C), jnp.float32), -4.0, 4.0)
    values = (noise + offsets) * rising[:, :, None, None]
    return values.astype(jnp.bfloat16)


def gaussian(own_key, extent, scale, most, held_as=jnp.bfloat16):
    array = scale * jax.random.normal(own_key, extent, jnp.float32)
    return jnp.clip(array, min=-most, max=most).astype(held_as)


def setup_inputs(seed: int = 0) -> dict:
    keys = jax.random.split(jax.random.key(seed), 10)
    return {
        "features": draw_features(jax.random.fold_in(keys[9], 71), 0),
        "gain_one": jnp.clip(1.0 + 0.18 * jax.random.normal(keys[1], (C,), jnp.float32), 0.1, 1.9),
        "shift_one": gaussian(keys[2], (C,), 0.3, 4.0, jnp.float32),
        "weight_one": gaussian(keys[3], (27 * C, C), (27 * C) ** -0.5, 0.109375),
        "bias_one": gaussian(keys[4], (C,), 0.5, 6.0, jnp.float32),
        "gain_two": jnp.clip(1.0 + 0.18 * jax.random.normal(keys[5], (C,), jnp.float32), 0.1, 1.9),
        "shift_two": gaussian(keys[6], (C,), 0.3, 4.0, jnp.float32),
        "weight_two": gaussian(keys[7], (27 * C, C), (27 * C) ** -0.5, 0.109375),
        "bias_two": gaussian(keys[8], (C,), 0.5, 6.0, jnp.float32),
    }


EPS = 1e-06

def group_moments(values):
    cell_count = values.shape[0] * values.shape[1] * values.shape[2] * (C // GROUPS)
    per_channel = lax.optimization_barrier(jnp.sum(values, axis=(0, 1, 2)))
    average = lax.optimization_barrier(jnp.sum(per_channel.reshape(GROUPS, -1), axis=1)) / cell_count
    centered = values - jnp.repeat(average, C // GROUPS)
    squares = lax.optimization_barrier(jnp.sum(centered * centered, axis=(0, 1, 2)))
    spread = lax.optimization_barrier(jnp.sum(squares.reshape(GROUPS, -1), axis=1)) / cell_count
    return (average, spread)

def activate(values, average, spread, gain, shift):
    center = jnp.repeat(average, C // GROUPS)
    factor = jnp.repeat(lax.rsqrt(spread + EPS), C // GROUPS)
    normed = (values - center) * factor * gain + shift
    return jax.nn.silu(normed).astype(jnp.bfloat16)

def causal_conv(activated, weight, bias):
    padded = jnp.concatenate([activated[:1], activated[:1], activated], 0)
    padded = jnp.pad(padded, ((0, 0), (1, 1), (1, 1), (0, 0)))

    def one_frame(frame):
        window = lax.dynamic_slice_in_dim(padded, frame, 3, 0)
        summed = jnp.zeros((H * W, C), jnp.float32)
        for time_tap in range(3):
            for row_tap in range(3):
                columns = jnp.concatenate([window[time_tap, row_tap:row_tap + H, col_tap:col_tap + W] for col_tap in range(3)], -1)
                first_row = (time_tap * 3 + row_tap) * 3 * C
                taps_block = weight[first_row:first_row + 3 * C]
                summed = summed + jnp.dot(columns.reshape(H * W, 3 * C), taps_block, preferred_element_type=jnp.float32)
        return summed.reshape(H, W, C) + bias
    return lax.map(one_frame, jnp.arange(NT, dtype=jnp.int32))

def reference(features, gain_one, shift_one, weight_one, bias_one, gain_two, shift_two, weight_two, bias_two):
    inputs = features.astype(jnp.float32)
    average, spread = group_moments(inputs)
    activated = activate(inputs, average, spread, gain_one, shift_one)
    hidden = causal_conv(activated, weight_one, bias_one).astype(jnp.bfloat16)
    hidden_wide = hidden.astype(jnp.float32)
    average_two, spread_two = group_moments(hidden_wide)
    second = activate(hidden_wide, average_two, spread_two, gain_two, shift_two)
    result = causal_conv(second, weight_two, bias_two) + inputs
    return result.astype(jnp.bfloat16)
```

```python
import jax
import jax.numpy as jnp
from jax import lax
from jax.sharding import Mesh
from jax.sharding import PartitionSpec as P

C = 128
GROUPS = 32
TM = ("y", "c")
ROWS = ("z", "x")
FAR = ("y", "z", "x")
EPS = 1e-06


def total_over_mesh(array):
    swapped = lax.ppermute(array, "c", [(0, 1), (1, 0)])
    pair = array + swapped
    count = lax.axis_size(FAR)
    copies = jnp.broadcast_to(pair, (count, *pair.shape))
    return lax.all_to_all(copies, FAR, split_axis=0, concat_axis=0, tiled=True).sum(axis=0)


def moments(values, cell_count):
    per_channel = jnp.stack([jnp.sum(values, axis=(0, 1, 2)), jnp.sum(values * values, axis=(0, 1, 2))])
    total = total_over_mesh(per_channel)
    first_sum, square_sum = jnp.sum(total.reshape(2, GROUPS, -1), axis=2)
    average = first_sum / cell_count
    spread = square_sum / cell_count - average * average
    return average, spread


def activate(values, average, spread, gain, shift):
    center = jnp.repeat(average, C // GROUPS)
    factor = jnp.repeat(lax.rsqrt(spread + EPS), C // GROUPS)
    normed = (values.astype(jnp.float32) - center) * factor * gain + shift
    return jax.nn.silu(normed).astype(jnp.bfloat16)


def sent(block, tm_step, row_step):
    tms, rows = lax.axis_size(TM), lax.axis_size(ROWS)
    route = []
    for t in range(tms):
        for r in range(rows):
            if 0 <= t + tm_step < tms and 0 <= r + row_step < rows:
                route.append((t * rows + r, (t + tm_step) * rows + r + row_step))
    return lax.ppermute(block, TM + ROWS, route)


def extended(block):
    top, bottom = block[:, :1], block[:, -1:]
    above = sent(bottom, 0, 1)
    below = sent(top, 0, -1)
    back = sent(block[-2:], 1, 0)
    back_above = sent(bottom[-2:], 1, 1)
    back_below = sent(top[-2:], 1, -1)
    now = jnp.concatenate([above, block, below], 1)
    before = jnp.concatenate([back_above, back, back_below], 1)
    repeated = jnp.broadcast_to(now[:1], before.shape)
    before = jnp.where(lax.axis_index(TM) == 0, repeated, before)
    return jnp.concatenate([before, now], 0)


def zero_outside(block):
    row = lax.axis_index(ROWS)
    index = lax.broadcasted_iota(jnp.int32, block.shape, 1)
    first = jnp.where(row == 0, 1, 0)
    last = jnp.where(row == lax.axis_size(ROWS) - 1, block.shape[1] - 1, block.shape[1])
    return jnp.where((index >= first) & (index < last), block, jnp.zeros_like(block))


def valid_conv(padded, weight, bias):
    out_frames, out_rows = padded.shape[0] - 2, padded.shape[1] - 2
    width_cells, channels = padded.shape[2], padded.shape[3]
    widened = jnp.pad(padded, ((0, 0), (0, 0), (1, 1), (0, 0)))
    summed = jnp.zeros((out_frames, out_rows, width_cells, channels), jnp.float32)
    for time_tap in range(3):
        for row_tap in range(3):
            columns = jnp.concatenate(
                [
                    widened[
                        time_tap : time_tap + out_frames,
                        row_tap : row_tap + out_rows,
                        col_tap : col_tap + width_cells,
                    ]
                    for col_tap in range(3)
                ],
                -1,
            )
            first_row = (time_tap * 3 + row_tap) * 3 * channels
            taps_block = weight[first_row : first_row + 3 * channels]
            summed = summed + jnp.einsum(
                "frwk,kc->frwc", columns, taps_block, preferred_element_type=jnp.float32
            )
    return summed + bias


def body(features, gain_one, shift_one, weight_one, bias_one, gain_two, shift_two, weight_two, bias_two):
    inputs = features.astype(jnp.float32)
    cell_count = (
        features.shape[0] * features.shape[1] * features.shape[2] * (C // GROUPS)
        * lax.axis_size(TM) * lax.axis_size(ROWS)
    )
    wide = extended(features)
    average, spread = moments(inputs, cell_count)
    activated = zero_outside(activate(wide, average, spread, gain_one, shift_one))
    hidden = valid_conv(activated, weight_one, bias_one).astype(jnp.bfloat16)
    hidden_wide = extended(hidden)
    average_two, spread_two = moments(hidden.astype(jnp.float32), cell_count)
    second = zero_outside(activate(hidden_wide, average_two, spread_two, gain_two, shift_two))
    result = valid_conv(second, weight_two, bias_two) + inputs
    return result.astype(jnp.bfloat16)


def solution(mesh):
    split = Mesh(mesh.devices.reshape(4, 2, 8, 4), ("y", "c", "z", "x"))
    return jax.shard_map(
        body,
        mesh=split,
        in_specs=(P(TM, ROWS, None, None), P(), P(), P(), P(), P(), P(), P(), P()),
        out_specs=P(TM, ROWS, None, None),
        check_vma=False,
    )
```

```python
import jax
import jax.numpy as jnp
from jax import lax
from jax.experimental import pallas as pl
from jax.experimental.pallas import tpu as pltpu
from jax.sharding import Mesh
from jax.sharding import PartitionSpec as P

C = 128
GROUP = 4
TM = ("y", "c")
ROWS = ("z", "x")
EVERY = TM + ROWS
EPS = 1e-06
MIB = 1 << 20
VMEM = pl.BlockSpec(memory_space=pltpu.VMEM)
SMEM = pl.BlockSpec(memory_space=pltpu.SMEM)


def group_total(v):
    lane = lax.broadcasted_iota(jnp.int32, v.shape, v.ndim - 1)
    for step in (1, 2):
        ahead = pltpu.roll(v, C - step, v.ndim - 1)
        behind = pltpu.roll(v, step, v.ndim - 1)
        v = v + jnp.where((lane & step) == 0, ahead, behind)
    return v


def local_sums(ref, frames, rows, width):
    cells = frames * rows * width

    def over(step):
        total = jnp.zeros((8, C), jnp.float32)
        for f in range(frames):
            for r in range(rows):
                part = step(ref[f, r].astype(jnp.float32))
                total = total + part.reshape(width // 8, 8, C).sum(axis=0)
        return jnp.sum(total, axis=0, keepdims=True)

    first = over(lambda v: v)
    mean = first / cells
    centered = over(lambda v: (v - mean) * (v - mean))
    return first, centered


def scale_and_offset(sums_ref, gain_ref, shift_ref, cells):
    devices = sums_ref.shape[0]
    every = sums_ref[:, 0, :]
    squares = jnp.sum(sums_ref[:, 1, :], axis=0, keepdims=True)
    whole = cells * devices * GROUP
    average = group_total(jnp.broadcast_to(jnp.sum(every, axis=0, keepdims=True), (8, C)))[:1] / whole
    apart = every / cells - average
    squares = squares + cells * jnp.sum(apart * apart, axis=0, keepdims=True)
    spread = group_total(jnp.broadcast_to(squares, (8, C)))[:1] / whole
    scale = lax.rsqrt(spread + EPS) * gain_ref[...]
    offset = shift_ref[...] - average * scale
    return 0.5 * scale, 0.5 * offset


def activated(values, scale, offset):
    half = values.astype(jnp.float32) * scale + offset
    return (half + half * jnp.tanh(half)).astype(jnp.bfloat16)


def fill(act_ref, own, back, above_ref, below_ref, flags_ref, scale, offset):
    back_frames = 2
    frames, rows, width = act_ref.shape[0], act_ref.shape[1], act_ref.shape[2]
    for f in range(frames):
        act_ref[f, 0] = activated(above_ref[f, 0], scale, offset)
        act_ref[f, rows - 1] = activated(below_ref[f, 0], scale, offset)
        for r in range(1, rows - 1):
            source = back(f, r - 1) if f < back_frames else own(f - back_frames, r - 1)
            act_ref[f, r] = activated(source, scale, offset)

    @pl.when(flags_ref[1] == 1)
    def _():
        act_ref[:, 0] = jnp.zeros((frames, width, C), jnp.bfloat16)

    @pl.when(flags_ref[2] == 1)
    def _():
        act_ref[:, rows - 1] = jnp.zeros((frames, width, C), jnp.bfloat16)

    @pl.when(flags_ref[0] == 1)
    def _():
        act_ref[0] = act_ref[back_frames]
        act_ref[1] = act_ref[back_frames]


def taps(act_ref, w_ref, start, count):
    width = act_ref.shape[2]
    cells = count * width
    pieces = [
        act_ref[start + i : start + i + count, r].reshape(cells, C) for i in range(3) for r in range(4)
    ]
    left = jnp.concatenate(pieces, axis=1)
    column = lax.broadcasted_iota(jnp.int32, (cells, 2 * C), 0) % width

    def block(i, j, k):
        if not 0 <= j < 3:
            return jnp.zeros((C, C), jnp.bfloat16)
        first = ((i * 3 + j) * 3 + k) * C
        return w_ref[first : first + C, :]

    total = None
    for k in (1, 0, 2):
        right = jnp.concatenate(
            [
                jnp.concatenate([block(i, r, k), block(i, r - 1, k)], axis=1)
                for i in range(3)
                for r in range(4)
            ],
            axis=0,
        )
        part = jnp.dot(left, right, preferred_element_type=jnp.float32)
        if k == 0:
            part = jnp.where(column == 0, 0.0, pltpu.roll(part, 1, 0))
        if k == 2:
            part = jnp.where(column == width - 1, 0.0, pltpu.roll(part, cells - 1, 0))
        total = part if total is None else total + part
    return total


def stats_kernel(x_ref, sums_ref):
    frames, rows, width, _ = x_ref.shape
    first, centered = local_sums(x_ref, frames, rows, width)
    pair = jnp.concatenate([first, centered], axis=0)
    sums_ref[...] = jnp.broadcast_to(pair[None], sums_ref.shape)


def first_conv_kernel(
    flags_ref, own_ref, back_ref, above_ref, below_ref, sums_ref, gain_ref, shift_ref, w_ref, bias_ref,
    hidden_ref, next_ref, act_ref,
):
    frames, rows, width, _ = own_ref.shape
    scale, offset = scale_and_offset(sums_ref, gain_ref, shift_ref, frames * rows * width)
    fill(
        act_ref, lambda f, r: own_ref[f, r], lambda f, r: back_ref[f, r], above_ref, below_ref,
        flags_ref, scale, offset,
    )
    for f in range(frames):
        total = taps(act_ref, w_ref, f, 1)
        for r in range(rows):
            value = total[:, r * C : (r + 1) * C] + bias_ref[...]
            hidden_ref[f, r] = value.astype(jnp.bfloat16)
    first, centered = local_sums(hidden_ref, frames, rows, width)
    pair = jnp.concatenate([first, centered], axis=0)
    next_ref[...] = jnp.broadcast_to(pair[None], next_ref.shape)


def second_conv_kernel(
    flags_ref, own_ref, back_ref, above_ref, below_ref, sums_ref, gain_ref, shift_ref, w_ref, bias_ref,
    features_ref, out_ref, act_ref,
):
    frames, rows, width, _ = own_ref.shape
    scale, offset = scale_and_offset(sums_ref, gain_ref, shift_ref, frames * rows * width)
    fill(
        act_ref, lambda f, r: own_ref[f, r], lambda f, r: back_ref[f, r], above_ref, below_ref,
        flags_ref, scale, offset,
    )
    for f in range(frames):
        total = taps(act_ref, w_ref, f, 1)
        for r in range(rows):
            value = total[:, r * C : (r + 1) * C] + bias_ref[...]
            value = value + features_ref[f, r].astype(jnp.float32)
            out_ref[f, r] = value.astype(jnp.bfloat16)


def edge_kernel(own_ref, back_ref, top_ref, bottom_ref):
    rows = own_ref.shape[1]
    top_ref[:2, 0] = back_ref[:, 0]
    top_ref[2:, 0] = own_ref[:, 0]
    bottom_ref[:2, 0] = back_ref[:, rows - 1]
    bottom_ref[2:, 0] = own_ref[:, rows - 1]


def shifted(block, axes, step):
    count = lax.axis_size(axes)
    return lax.ppermute(block, axes, [(i, i + step) for i in range(count) if 0 <= i + step < count])


def edges(own, back):
    frames, _, width, _ = own.shape
    shape = jax.ShapeDtypeStruct((frames + 2, 1, width, C), own.dtype)
    top, bottom = pl.pallas_call(
        edge_kernel, out_shape=(shape, shape), in_specs=[VMEM] * 2, out_specs=(VMEM, VMEM), name="edge_rows",
        compiler_params=pltpu.CompilerParams(vmem_limit_bytes=8 * MIB),
    )(own, back)
    above = shifted(bottom, ROWS, 1)
    below = shifted(top, ROWS, -1)
    return above, below


def everywhere(copies):
    return lax.all_to_all(copies, EVERY, split_axis=0, concat_axis=0, tiled=True)


def body(features, gain_one, shift_one, weight_one, bias_one, gain_two, shift_two, weight_two, bias_two):
    frames, rows, width, _ = features.shape
    devices = lax.axis_size(EVERY)
    copies = jax.ShapeDtypeStruct((devices, 2, C), jnp.float32)
    row = lax.axis_index(ROWS)
    flags = jnp.stack(
        [lax.axis_index(TM) == 0, row == 0, row == lax.axis_size(ROWS) - 1]
    ).astype(jnp.int32)
    scratch = [pltpu.VMEM((frames + 2, rows + 2, width, C), jnp.bfloat16)]
    specs = [SMEM] + [VMEM] * 9
    vectors = [v.reshape(1, C) for v in (gain_one, shift_one, bias_one, gain_two, shift_two, bias_two)]

    back = shifted(features[-2:], TM, 1)
    sums = pl.pallas_call(
        stats_kernel, out_shape=copies, in_specs=[VMEM], out_specs=VMEM, name="moments",
        compiler_params=pltpu.CompilerParams(vmem_limit_bytes=8 * MIB),
    )(features)
    above, below = edges(features, back)
    sums = everywhere(sums)
    hidden, sums_two = pl.pallas_call(
        first_conv_kernel,
        out_shape=(jax.ShapeDtypeStruct(features.shape, jnp.bfloat16), copies),
        in_specs=specs,
        out_specs=(VMEM, VMEM),
        scratch_shapes=scratch,
        compiler_params=pltpu.CompilerParams(vmem_limit_bytes=32 * MIB),
        name="first_conv",
    )(flags, features, back, above, below, sums, vectors[0], vectors[1], weight_one, vectors[2])

    back = shifted(hidden[-2:], TM, 1)
    above, below = edges(hidden, back)
    sums_two = everywhere(sums_two)
    return pl.pallas_call(
        second_conv_kernel,
        out_shape=jax.ShapeDtypeStruct(features.shape, jnp.bfloat16),
        in_specs=specs + [VMEM],
        out_specs=VMEM,
        scratch_shapes=scratch,
        compiler_params=pltpu.CompilerParams(vmem_limit_bytes=32 * MIB),
        name="second_conv",
    )(flags, hidden, back, above, below, sums_two, vectors[3], vectors[4], weight_two, vectors[5], features)


def solution(mesh):
    split = Mesh(mesh.devices.reshape(4, 2, 8, 4), EVERY)
    return jax.shard_map(
        body,
        mesh=split,
        in_specs=(P(TM, ROWS, None, None), P(), P(), P(), P(), P(), P(), P(), P()),
        out_specs=P(TM, ROWS, None, None),
        check_vma=False,
    )
```

```python
import jax
import jax.numpy as jnp
from jax import lax
from jax.experimental import pallas as pl
from jax.experimental.pallas import tpu as pltpu
from jax.sharding import Mesh
from jax.sharding import PartitionSpec as P

C = 128
GROUP = 4
TM = ("y", "c")
ROWS = ("z", "x")
EVERY = TM + ROWS
EPS = 1e-06
MIB = 1 << 20
VMEM = pl.BlockSpec(memory_space=pltpu.VMEM)
SMEM = pl.BlockSpec(memory_space=pltpu.SMEM)


def group_total(v):
    lane = lax.broadcasted_iota(jnp.int32, v.shape, v.ndim - 1)
    for step in (1, 2):
        ahead = pltpu.roll(v, C - step, v.ndim - 1)
        behind = pltpu.roll(v, step, v.ndim - 1)
        v = v + jnp.where((lane & step) == 0, ahead, behind)
    return v


def packed_sums(ref):
    frames, rows, width, _ = ref.shape
    cells = frames * rows * width * GROUP

    def over(step):
        total = jnp.zeros((8, C), jnp.float32)
        for f in range(frames):
            for r in range(rows):
                part = step(ref[f, r].astype(jnp.float32))
                total = total + part.reshape(width // 8, 8, C).sum(axis=0)
        return group_total(jnp.broadcast_to(jnp.sum(total, axis=0, keepdims=True), (8, C)))

    first = over(lambda v: v)
    mean = first[:1] / cells
    centered = over(lambda v: (v - mean) * (v - mean))
    place = lax.broadcasted_iota(jnp.int32, (8, C), 1) % GROUP
    return jnp.where(place == 0, first, jnp.where(place == 1, centered, 0.0))


def scale_and_offset(sums_ref, gain_ref, shift_ref, cells):
    devices = sums_ref.shape[0]
    cells = cells * GROUP
    place = lax.broadcasted_iota(jnp.int32, (8, C), 1) % GROUP

    def whole(rows):
        total = jnp.sum(rows.reshape(devices // 8, 8, C), axis=0)
        total = jnp.broadcast_to(jnp.sum(total, axis=0, keepdims=True), (8, C))
        return total

    every = sums_ref[...]
    total = whole(every)
    average = group_total(jnp.where(place == 0, total, 0.0)) / (cells * devices)
    apart = every / cells - average[:1]
    between = whole(apart * apart) * cells
    squares = jnp.where(place == 0, between, jnp.where(place == 1, total, 0.0))
    spread = group_total(squares) / (cells * devices)
    scale = lax.rsqrt(spread[:1] + EPS) * gain_ref[...]
    offset = shift_ref[...] - average[:1] * scale
    return 0.5 * scale, 0.5 * offset


def activated(values, scale, offset):
    half = values.astype(jnp.float32) * scale + offset
    return (half + half * jnp.tanh(half)).astype(jnp.bfloat16)


def fill(act_ref, own_ref, back_ref, above_ref, below_ref, flags_ref, scale, offset):
    earlier = back_ref.shape[0]
    frames, rows, width = act_ref.shape[0], act_ref.shape[1], act_ref.shape[2]
    for f in range(frames):
        for r in range(rows):
            if f < earlier:
                source = back_ref[f, r]
            elif r == 0:
                source = above_ref[f - earlier, 0]
            elif r == rows - 1:
                source = below_ref[f - earlier, 0]
            else:
                source = own_ref[f - earlier, r - 1]
            act_ref[f, r] = activated(source, scale, offset)

    @pl.when(flags_ref[1] == 1)
    def _():
        act_ref[:, 0] = jnp.zeros((frames, width, C), jnp.bfloat16)

    @pl.when(flags_ref[2] == 1)
    def _():
        act_ref[:, rows - 1] = jnp.zeros((frames, width, C), jnp.bfloat16)

    @pl.when(flags_ref[0] == 1)
    def _():
        for f in range(earlier):
            act_ref[f] = act_ref[earlier]


def taps(act_ref, w_ref, start, count):
    width = act_ref.shape[2]
    cells = count * width
    pieces = [
        act_ref[start + i : start + i + count, r].reshape(cells, C) for i in range(3) for r in range(4)
    ]
    left = jnp.concatenate(pieces, axis=1)
    column = lax.broadcasted_iota(jnp.int32, (cells, 2 * C), 0) % width

    def block(i, j, k):
        if not 0 <= j < 3:
            return jnp.zeros((C, C), jnp.bfloat16)
        first = ((i * 3 + j) * 3 + k) * C
        return w_ref[first : first + C, :]

    total = None
    for k in (1, 0, 2):
        right = jnp.concatenate(
            [
                jnp.concatenate([block(i, r, k), block(i, r - 1, k)], axis=1)
                for i in range(3)
                for r in range(4)
            ],
            axis=0,
        )
        part = jnp.dot(left, right, preferred_element_type=jnp.float32)
        if k == 0:
            part = jnp.where(column == 0, 0.0, pltpu.roll(part, 1, 0))
        if k == 2:
            part = jnp.where(column == width - 1, 0.0, pltpu.roll(part, cells - 1, 0))
        total = part if total is None else total + part
    return total


def hand_out(ref, top_ref, bottom_ref, sums_ref):
    rows = ref.shape[1]
    top_ref[:, 0] = ref[:, 0]
    bottom_ref[:, 0] = ref[:, rows - 1]
    sums_ref[...] = jnp.broadcast_to(packed_sums(ref)[:1], sums_ref.shape)


def moments_kernel(x_ref, top_ref, bottom_ref, sums_ref):
    hand_out(x_ref, top_ref, bottom_ref, sums_ref)


def first_conv_kernel(
    flags_ref, own_ref, back_ref, above_ref, below_ref, sums_ref, gain_ref, shift_ref, w_ref, bias_ref,
    hidden_ref, top_ref, bottom_ref, next_ref, act_ref,
):
    frames, rows, width, _ = own_ref.shape
    scale, offset = scale_and_offset(sums_ref, gain_ref, shift_ref, frames * rows * width)
    fill(act_ref, own_ref, back_ref, above_ref, below_ref, flags_ref, scale, offset)
    for f in range(frames):
        total = taps(act_ref, w_ref, f, 1)
        for r in range(rows):
            value = total[:, r * C : (r + 1) * C] + bias_ref[...]
            hidden_ref[f, r] = value.astype(jnp.bfloat16)
    hand_out(hidden_ref, top_ref, bottom_ref, next_ref)


def second_conv_kernel(
    flags_ref, own_ref, back_ref, above_ref, below_ref, sums_ref, gain_ref, shift_ref, w_ref, bias_ref,
    features_ref, out_ref, act_ref,
):
    frames, rows, width, _ = own_ref.shape
    scale, offset = scale_and_offset(sums_ref, gain_ref, shift_ref, frames * rows * width)
    fill(act_ref, own_ref, back_ref, above_ref, below_ref, flags_ref, scale, offset)
    for f in range(frames):
        total = taps(act_ref, w_ref, f, 1)
        for r in range(rows):
            value = total[:, r * C : (r + 1) * C] + bias_ref[...]
            value = value + features_ref[f, r].astype(jnp.float32)
            out_ref[f, r] = value.astype(jnp.bfloat16)


def last_kernel(own_ref, above_ref, below_ref, last_ref):
    earlier, rows = last_ref.shape[0], last_ref.shape[1]
    for f in range(earlier):
        source = own_ref.shape[0] - earlier + f
        last_ref[f, 0] = above_ref[source, 0]
        last_ref[f, 1 : rows - 1] = own_ref[source]
        last_ref[f, rows - 1] = below_ref[source, 0]


def shifted(block, axes, step):
    count = lax.axis_size(axes)
    return lax.ppermute(block, axes, [(i, i + step) for i in range(count) if 0 <= i + step < count])


def neighbours(own, top, bottom):
    _, rows, width, _ = own.shape
    above = shifted(bottom, ROWS, 1)
    below = shifted(top, ROWS, -1)
    last = pl.pallas_call(
        last_kernel,
        out_shape=jax.ShapeDtypeStruct((2, rows + 2, width, C), own.dtype),
        in_specs=[VMEM] * 3,
        out_specs=VMEM,
        name="last_frames",
        compiler_params=pltpu.CompilerParams(vmem_limit_bytes=8 * MIB),
    )(own, above, below)
    back = shifted(last, TM, 1)
    return back, above, below


def everywhere(copies):
    devices = copies.shape[0]
    received = lax.all_to_all(
        copies.reshape(devices, 1, C), EVERY, split_axis=0, concat_axis=0, tiled=True
    )
    return received.reshape(devices, C)


def body(features, gain_one, shift_one, weight_one, bias_one, gain_two, shift_two, weight_two, bias_two):
    frames, rows, width, _ = features.shape
    copies = jax.ShapeDtypeStruct((lax.axis_size(EVERY), C), jnp.float32)
    tile = jax.ShapeDtypeStruct(features.shape, jnp.bfloat16)
    edge = jax.ShapeDtypeStruct((frames, 1, width, C), jnp.bfloat16)
    row = lax.axis_index(ROWS)
    flags = jnp.stack(
        [lax.axis_index(TM) == 0, row == 0, row == lax.axis_size(ROWS) - 1]
    ).astype(jnp.int32)
    common = dict(
        scratch_shapes=[pltpu.VMEM((frames + 2, rows + 2, width, C), jnp.bfloat16)],
        compiler_params=pltpu.CompilerParams(vmem_limit_bytes=32 * MIB),
    )
    specs = [SMEM] + [VMEM] * 9
    vectors = [v.reshape(1, C) for v in (gain_one, shift_one, bias_one, gain_two, shift_two, bias_two)]

    top, bottom, sums = pl.pallas_call(
        moments_kernel,
        out_shape=(edge, edge, copies),
        in_specs=[VMEM],
        out_specs=(VMEM,) * 3,
        name="moments",
        compiler_params=pltpu.CompilerParams(vmem_limit_bytes=8 * MIB),
    )(features)
    back, above, below = neighbours(features, top, bottom)
    sums = everywhere(sums)
    hidden, top, bottom, sums_two = pl.pallas_call(
        first_conv_kernel,
        out_shape=(tile, edge, edge, copies),
        in_specs=specs,
        out_specs=(VMEM,) * 4,
        name="first_conv",
        **common,
    )(flags, features, back, above, below, sums, vectors[0], vectors[1], weight_one, vectors[2])

    back, above, below = neighbours(hidden, top, bottom)
    sums_two = everywhere(sums_two)
    return pl.pallas_call(
        second_conv_kernel,
        out_shape=tile,
        in_specs=specs + [VMEM],
        out_specs=VMEM,
        name="second_conv",
        **common,
    )(flags, hidden, back, above, below, sums_two, vectors[3], vectors[4], weight_two, vectors[5], features)


def solution(mesh):
    split = Mesh(mesh.devices.reshape(4, 2, 8, 4), EVERY)
    return jax.shard_map(
        body,
        mesh=split,
        in_specs=(P(TM, ROWS, None, None), P(), P(), P(), P(), P(), P(), P(), P()),
        out_specs=P(TM, ROWS, None, None),
        check_vma=False,
    )
```

```python
import functools

import jax
import jax.numpy as jnp
from jax import lax
from jax.experimental import pallas as pl
from jax.experimental.pallas import tpu as pltpu
from jax.sharding import Mesh
from jax.sharding import PartitionSpec as P

C = 128
GROUP = 4
TM = ("y", "c")
ROWS = ("z", "x")
EVERY = TM + ROWS
FAR = ("y", "z")
NEAR = ("c", "x")
EPS = 1e-06
MIB = 1 << 20
VMEM = pl.BlockSpec(memory_space=pltpu.VMEM)
SMEM = pl.BlockSpec(memory_space=pltpu.SMEM)


def group_total(v):
    lane = lax.broadcasted_iota(jnp.int32, v.shape, v.ndim - 1)
    for step in (1, 2):
        ahead = pltpu.roll(v, C - step, v.ndim - 1)
        behind = pltpu.roll(v, step, v.ndim - 1)
        v = v + jnp.where((lane & step) == 0, ahead, behind)
    return v


def lane_place(shape):
    return lax.broadcasted_iota(jnp.int32, shape, len(shape) - 1) % GROUP


def packed(first, centered):
    place = lane_place(first.shape)
    return jnp.where(place == 0, first, jnp.where(place == 1, centered, 0.0))


def column_total(rows):
    total = jnp.sum(rows.reshape(rows.shape[0] // 8, 8, C), axis=0)
    return jnp.broadcast_to(jnp.sum(total, axis=0, keepdims=True), (8, C))


def packed_sums(ref):
    frames, rows, width, _ = ref.shape
    cells = frames * rows * width * GROUP

    def over(step):
        total = jnp.zeros((8, C), jnp.float32)
        for f in range(frames):
            for r in range(rows):
                part = step(ref[f, r].astype(jnp.float32))
                total = total + part.reshape(width // 8, 8, C).sum(axis=0)
        return group_total(column_total(total))

    first = over(lambda v: v)
    mean = first[:1] / cells
    return packed(first, over(lambda v: (v - mean) * (v - mean)))


def merged(every, cells):
    count = every.shape[0]
    total = column_total(every)
    place = lane_place(total.shape)
    first = group_total(jnp.where(place == 0, total, 0.0))
    apart = every / cells - first[:1] / (cells * count)
    between = column_total(apart * apart) * cells
    centered = group_total(jnp.where(place == 0, between, jnp.where(place == 1, total, 0.0)))
    return first, centered


def scale_and_offset(sums_ref, vectors_ref, which, tile_cells, devices):
    count = sums_ref.shape[0]
    cells = tile_cells * GROUP * devices
    first, centered = merged(sums_ref[...], cells // count)
    average, spread = first[:1] / cells, centered[:1] / cells
    scale = lax.rsqrt(spread + EPS) * vectors_ref[which : which + 1]
    offset = vectors_ref[which + 1 : which + 2] - average * scale
    return 0.5 * scale, 0.5 * offset


def activated(values, scale, offset):
    half = values.astype(jnp.float32) * scale + offset
    return (half + half * jnp.tanh(half)).astype(jnp.bfloat16)


def fill(act_ref, own_ref, back_ref, above_ref, below_ref, flags_ref, scale, offset):
    earlier = back_ref.shape[0]
    frames, rows, width = act_ref.shape[0], act_ref.shape[1], act_ref.shape[2]
    for f in range(frames):
        for r in range(rows):
            if f < earlier:
                source = back_ref[f, r]
            elif r == 0:
                source = above_ref[f - earlier, 0]
            elif r == rows - 1:
                source = below_ref[f - earlier, 0]
            else:
                source = own_ref[f - earlier, r - 1]
            act_ref[f, r] = activated(source, scale, offset)

    @pl.when(flags_ref[1] == 1)
    def _():
        act_ref[:, 0] = jnp.zeros((frames, width, C), jnp.bfloat16)

    @pl.when(flags_ref[2] == 1)
    def _():
        act_ref[:, rows - 1] = jnp.zeros((frames, width, C), jnp.bfloat16)

    @pl.when(flags_ref[0] == 1)
    def _():
        for f in range(earlier):
            act_ref[f] = act_ref[earlier]


def taps(act_ref, w_ref, start, count):
    width = act_ref.shape[2]
    cells = count * width
    pieces = [
        act_ref[start + i : start + i + count, r].reshape(cells, C) for i in range(3) for r in range(4)
    ]
    left = jnp.concatenate(pieces, axis=1)
    column = lax.broadcasted_iota(jnp.int32, (cells, 2 * C), 0) % width

    def block(i, j, k):
        if not 0 <= j < 3:
            return jnp.zeros((C, C), jnp.bfloat16)
        first = ((i * 3 + j) * 3 + k) * C
        return w_ref[first : first + C, :]

    total = None
    for k in (1, 0, 2):
        right = jnp.concatenate(
            [
                jnp.concatenate([block(i, r, k), block(i, r - 1, k)], axis=1)
                for i in range(3)
                for r in range(4)
            ],
            axis=0,
        )
        part = jnp.dot(left, right, preferred_element_type=jnp.float32)
        if k == 0:
            part = jnp.where(column == 0, 0.0, pltpu.roll(part, 1, 0))
        if k == 2:
            part = jnp.where(column == width - 1, 0.0, pltpu.roll(part, cells - 1, 0))
        total = part if total is None else total + part
    return total


def hand_out(ref, top_ref, bottom_ref, sums_ref):
    rows = ref.shape[1]
    top_ref[:, 0] = ref[:, 0]
    bottom_ref[:, 0] = ref[:, rows - 1]
    sums_ref[...] = jnp.broadcast_to(packed_sums(ref)[:1], sums_ref.shape)


def moments_kernel(x_ref, *refs):
    vectors, (top_ref, bottom_ref, sums_ref, vectors_ref) = refs[:-4], refs[-4:]
    hand_out(x_ref, top_ref, bottom_ref, sums_ref)
    for i, vector in enumerate(vectors):
        vectors_ref[i : i + 1] = vector[...]


def relay_kernel(cells, sums_ref, next_ref):
    both = packed(*merged(sums_ref[...], cells))
    next_ref[...] = jnp.broadcast_to(both[:1], next_ref.shape)


def first_conv_kernel(
    devices, flags_ref, own_ref, back_ref, above_ref, below_ref, sums_ref, vectors_ref, w_ref,
    hidden_ref, top_ref, bottom_ref, next_ref, act_ref,
):
    frames, rows, width, _ = own_ref.shape
    scale, offset = scale_and_offset(sums_ref, vectors_ref, 0, frames * rows * width, devices)
    fill(act_ref, own_ref, back_ref, above_ref, below_ref, flags_ref, scale, offset)
    for f in range(frames):
        total = taps(act_ref, w_ref, f, 1)
        for r in range(rows):
            value = total[:, r * C : (r + 1) * C] + vectors_ref[2:3]
            hidden_ref[f, r] = value.astype(jnp.bfloat16)
    hand_out(hidden_ref, top_ref, bottom_ref, next_ref)


def second_conv_kernel(
    devices, flags_ref, own_ref, back_ref, above_ref, below_ref, sums_ref, vectors_ref, w_ref,
    features_ref, out_ref, act_ref,
):
    frames, rows, width, _ = own_ref.shape
    scale, offset = scale_and_offset(sums_ref, vectors_ref, 3, frames * rows * width, devices)
    fill(act_ref, own_ref, back_ref, above_ref, below_ref, flags_ref, scale, offset)
    for f in range(frames):
        total = taps(act_ref, w_ref, f, 1)
        for r in range(rows):
            value = total[:, r * C : (r + 1) * C] + vectors_ref[5:6]
            value = value + features_ref[f, r].astype(jnp.float32)
            out_ref[f, r] = value.astype(jnp.bfloat16)


def last_kernel(own_ref, above_ref, below_ref, last_ref):
    earlier, rows = last_ref.shape[0], last_ref.shape[1]
    for f in range(earlier):
        source = own_ref.shape[0] - earlier + f
        last_ref[f, 0] = above_ref[source, 0]
        last_ref[f, 1 : rows - 1] = own_ref[source]
        last_ref[f, rows - 1] = below_ref[source, 0]


def shifted(block, axes, step):
    count = lax.axis_size(axes)
    return lax.ppermute(block, axes, [(i, i + step) for i in range(count) if 0 <= i + step < count])


def neighbours(own, top, bottom):
    _, rows, width, _ = own.shape
    above = shifted(bottom, ROWS, 1)
    below = shifted(top, ROWS, -1)
    last = pl.pallas_call(
        last_kernel,
        out_shape=jax.ShapeDtypeStruct((2, rows + 2, width, C), own.dtype),
        in_specs=[VMEM] * 3,
        out_specs=VMEM,
        name="last_frames",
        compiler_params=pltpu.CompilerParams(vmem_limit_bytes=8 * MIB),
    )(own, above, below)
    back = shifted(last, TM, 1)
    return back, above, below


def exchanged(copies, axes):
    count = copies.shape[0]
    received = lax.all_to_all(copies.reshape(count, 1, C), axes, split_axis=0, concat_axis=0, tiled=True)
    return received.reshape(count, C)


def everywhere(copies, tile_cells):
    sums = exchanged(copies, FAR)
    copies = pl.pallas_call(
        functools.partial(relay_kernel, tile_cells * GROUP),
        out_shape=jax.ShapeDtypeStruct((lax.axis_size(NEAR), C), jnp.float32),
        in_specs=[VMEM],
        out_specs=VMEM,
        name="relay",
        compiler_params=pltpu.CompilerParams(vmem_limit_bytes=4 * MIB),
    )(sums)
    return exchanged(copies, NEAR)


def body(features, gain_one, shift_one, weight_one, bias_one, gain_two, shift_two, weight_two, bias_two):
    frames, rows, width, _ = features.shape
    copies = jax.ShapeDtypeStruct((lax.axis_size(FAR), C), jnp.float32)
    devices = lax.axis_size(EVERY)
    tile_cells = frames * rows * width
    tile = jax.ShapeDtypeStruct(features.shape, jnp.bfloat16)
    edge = jax.ShapeDtypeStruct((frames, 1, width, C), jnp.bfloat16)
    row = lax.axis_index(ROWS)
    flags = jnp.stack(
        [lax.axis_index(TM) == 0, row == 0, row == lax.axis_size(ROWS) - 1]
    ).astype(jnp.int32)
    common = dict(
        scratch_shapes=[pltpu.VMEM((frames + 2, rows + 2, width, C), jnp.bfloat16)],
        compiler_params=pltpu.CompilerParams(vmem_limit_bytes=32 * MIB),
    )
    specs = [SMEM] + [VMEM] * 7
    vectors = [v.reshape(1, C) for v in (gain_one, shift_one, bias_one, gain_two, shift_two, bias_two)]

    top, bottom, sums, vectors = pl.pallas_call(
        moments_kernel,
        out_shape=(edge, edge, copies, jax.ShapeDtypeStruct((8, C), jnp.float32)),
        in_specs=[VMEM] * 7,
        out_specs=(VMEM,) * 4,
        name="moments",
        compiler_params=pltpu.CompilerParams(vmem_limit_bytes=8 * MIB),
    )(features, *vectors)
    back, above, below = neighbours(features, top, bottom)
    sums = everywhere(sums, tile_cells)
    hidden, top, bottom, sums_two = pl.pallas_call(
        functools.partial(first_conv_kernel, devices),
        out_shape=(tile, edge, edge, copies),
        in_specs=specs,
        out_specs=(VMEM,) * 4,
        name="first_conv",
        **common,
    )(flags, features, back, above, below, sums, vectors, weight_one)

    back, above, below = neighbours(hidden, top, bottom)
    sums_two = everywhere(sums_two, tile_cells)
    return pl.pallas_call(
        functools.partial(second_conv_kernel, devices),
        out_shape=tile,
        in_specs=specs + [VMEM],
        out_specs=VMEM,
        name="second_conv",
        **common,
    )(flags, hidden, back, above, below, sums_two, vectors, weight_two, features)


def solution(mesh):
    split = Mesh(mesh.devices.reshape(4, 2, 8, 4), EVERY)
    return jax.shard_map(
        body,
        mesh=split,
        in_specs=(P(TM, ROWS, None, None), P(), P(), P(), P(), P(), P(), P(), P()),
        out_specs=P(TM, ROWS, None, None),
        check_vma=False,
    )
```

```python
import functools

import jax
import jax.numpy as jnp
from jax import lax
from jax.experimental import pallas as pl
from jax.experimental.pallas import tpu as pltpu
from jax.sharding import Mesh
from jax.sharding import PartitionSpec as P

C = 128
GROUP = 4
TM = ("y", "c")
ROWS = ("z", "x")
EVERY = TM + ROWS
FAR = ("y", "z")
NEAR = ("c", "x")
EPS = 1e-06
MIB = 1 << 20
VMEM = pl.BlockSpec(memory_space=pltpu.VMEM)
SMEM = pl.BlockSpec(memory_space=pltpu.SMEM)


def group_total(v):
    lane = lax.broadcasted_iota(jnp.int32, v.shape, v.ndim - 1)
    for step in (1, 2):
        ahead = pltpu.roll(v, C - step, v.ndim - 1)
        behind = pltpu.roll(v, step, v.ndim - 1)
        v = v + jnp.where((lane & step) == 0, ahead, behind)
    return v


def lane_place(shape):
    return lax.broadcasted_iota(jnp.int32, shape, len(shape) - 1) % GROUP


def packed(first, centered):
    place = lane_place(first.shape)
    return jnp.where(place == 0, first, jnp.where(place == 1, centered, 0.0))


def column_total(rows):
    total = jnp.sum(rows.reshape(rows.shape[0] // 8, 8, C), axis=0)
    return jnp.broadcast_to(jnp.sum(total, axis=0, keepdims=True), (8, C))


def packed_sums(ref):
    frames, rows, width, _ = ref.shape
    cells = frames * rows * width * GROUP

    def over(step):
        total = jnp.zeros((8, C), jnp.float32)
        for f in range(frames):
            for r in range(rows):
                part = step(ref[f, r].astype(jnp.float32))
                total = total + part.reshape(width // 8, 8, C).sum(axis=0)
        return group_total(column_total(total))

    first = over(lambda v: v)
    mean = first[:1] / cells
    return packed(first, over(lambda v: (v - mean) * (v - mean)))


def merged(every, cells):
    count = every.shape[0]
    total = column_total(every)
    place = lane_place(total.shape)
    first = group_total(jnp.where(place == 0, total, 0.0))
    apart = every / cells - first[:1] / (cells * count)
    between = column_total(apart * apart) * cells
    centered = group_total(jnp.where(place == 0, between, jnp.where(place == 1, total, 0.0)))
    return first, centered


def scale_and_offset(sums_ref, vectors_ref, which, tile_cells, devices):
    count = sums_ref.shape[0]
    cells = tile_cells * GROUP * devices
    first, centered = merged(sums_ref[...], cells // count)
    average, spread = first[:1] / cells, centered[:1] / cells
    scale = lax.rsqrt(spread + EPS) * vectors_ref[which : which + 1]
    offset = vectors_ref[which + 1 : which + 2] - average * scale
    return 0.5 * scale, 0.5 * offset


def activated(values, scale, offset):
    half = values.astype(jnp.float32) * scale + offset
    return (half + half * jnp.tanh(half)).astype(jnp.bfloat16)


def fill(act_ref, own_ref, rows_ref, back_ref, diagonal_ref, own_at, back_at, scale, offset):
    earlier, frames, rows = back_ref.shape[0], own_ref.shape[0], own_ref.shape[1]
    for r in range(rows):
        for f in range(earlier):
            act_ref[f, back_at + r] = activated(back_ref[f, r], scale, offset)
            act_ref[f, rows - back_at + r] = activated(diagonal_ref[f, r], scale, offset)
        for f in range(frames):
            act_ref[f + earlier, own_at + r] = activated(own_ref[f, r], scale, offset)
            act_ref[f + earlier, rows - own_at + r] = activated(rows_ref[f, r], scale, offset)


def repeat_first(act_ref, earlier):
    for f in range(earlier):
        act_ref[f] = act_ref[earlier]


def taps(act_ref, w_ref, start, count, wraps=None):
    width = act_ref.shape[2]
    cells = count * width
    pieces = [
        act_ref[start + i : start + i + count, r].reshape(cells, C) for i in range(3) for r in range(4)
    ]
    left = jnp.concatenate(pieces, axis=1)
    column = lax.broadcasted_iota(jnp.int32, (cells, 2 * C), 0) % width

    def block(i, r, out, k):
        j = r - out
        if not 0 <= j < 3:
            return jnp.zeros((C, C), jnp.bfloat16)
        first = ((i * 3 + j) * 3 + k) * C
        found = w_ref[first : first + C, :]
        if wraps is not None and r // 2 != out:
            return jnp.where(wraps, jnp.zeros_like(found), found)
        return found

    total = None
    for k in (1, 0, 2):
        right = jnp.concatenate(
            [
                jnp.concatenate([block(i, r, 0, k), block(i, r, 1, k)], axis=1)
                for i in range(3)
                for r in range(4)
            ],
            axis=0,
        )
        part = jnp.dot(left, right, preferred_element_type=jnp.float32)
        if k == 0:
            part = jnp.where(column == 0, 0.0, pltpu.roll(part, 1, 0))
        if k == 2:
            part = jnp.where(column == width - 1, 0.0, pltpu.roll(part, cells - 1, 0))
        total = part if total is None else total + part
    return total


def hand_out(ref, last_ref, sums_ref):
    earlier = last_ref.shape[0]
    last_ref[...] = ref[ref.shape[0] - earlier :]
    sums_ref[...] = jnp.broadcast_to(packed_sums(ref)[:1], sums_ref.shape)


def moments_kernel(x_ref, *refs):
    vectors, (last_ref, sums_ref, vectors_ref) = refs[:-3], refs[-3:]
    hand_out(x_ref, last_ref, sums_ref)
    for i, vector in enumerate(vectors):
        vectors_ref[i : i + 1] = vector[...]


def relay_kernel(cells, sums_ref, next_ref):
    both = packed(*merged(sums_ref[...], cells))
    next_ref[...] = jnp.broadcast_to(both[:1], next_ref.shape)


def first_conv_kernel(
    devices, place_ref, own_ref, rows_ref, back_ref, diagonal_ref, sums_ref, vectors_ref, w_ref,
    hidden_ref, last_ref, next_ref, act_ref,
):
    frames, rows, width, _ = own_ref.shape
    core, tm, row, last_row = place_ref[0], place_ref[1], place_ref[2], place_ref[3]
    side = rows * (1 - core)
    scale, offset = scale_and_offset(sums_ref, vectors_ref, 0, frames * rows * width, devices)
    fill(act_ref, own_ref, rows_ref, back_ref, diagonal_ref, side, side, scale, offset)

    @pl.when(tm == 0)
    def _():
        repeat_first(act_ref, back_ref.shape[0])

    wraps = row == core * last_row
    for f in range(frames):
        total = taps(act_ref, w_ref, f, 1, wraps)
        for r in range(rows):
            value = total[:, r * C : (r + 1) * C] + vectors_ref[2:3]
            hidden_ref[f, r] = value.astype(jnp.bfloat16)
    hand_out(hidden_ref, last_ref, next_ref)


def second_conv_kernel(
    devices, place_ref, own_ref, rows_ref, back_ref, diagonal_ref, sums_ref, vectors_ref, w_ref,
    features_ref, out_ref, act_ref,
):
    frames, rows, width, _ = own_ref.shape
    core, tm, row, last_row = place_ref[0], place_ref[1], place_ref[2], place_ref[3]
    scale, offset = scale_and_offset(sums_ref, vectors_ref, 3, frames * rows * width, devices)
    fill(
        act_ref, own_ref, rows_ref, back_ref, diagonal_ref, rows * core, rows * (1 - core), scale, offset
    )
    outside = jnp.zeros((act_ref.shape[0], width, C), jnp.bfloat16)

    @pl.when(row == 0)
    def _():
        act_ref[:, 0] = outside

    @pl.when(row == last_row)
    def _():
        act_ref[:, act_ref.shape[1] - 1] = outside

    @pl.when(tm == 0)
    def _():
        repeat_first(act_ref, back_ref.shape[0])

    for f in range(frames):
        total = taps(act_ref, w_ref, f, 1)
        for r in range(rows):
            value = total[:, r * C : (r + 1) * C] + vectors_ref[5:6]
            value = value + features_ref[f, r].astype(jnp.float32)
            out_ref[f, r] = value.astype(jnp.bfloat16)


def sent(block, tm_step, row_steps):
    tms, rows = lax.axis_size(TM), lax.axis_size(ROWS)
    route = []
    for t in range(tms):
        for r in range(rows):
            source = (t - tm_step, (r + row_steps[t % 2]) % rows)
            if source[0] >= 0:
                route.append((source[0] * rows + source[1], t * rows + r))
    return lax.ppermute(block, EVERY, route)


def neighbours(own, last, row_steps):
    beside = sent(own, 0, row_steps)
    back = sent(last, 1, (0, 0))
    diagonal = sent(last, 1, (-1, 1))
    return beside, back, diagonal


def exchanged(copies, axes):
    count = copies.shape[0]
    received = lax.all_to_all(copies.reshape(count, 1, C), axes, split_axis=0, concat_axis=0, tiled=True)
    return received.reshape(count, C)


def everywhere(copies, tile_cells):
    sums = exchanged(copies, FAR)
    copies = pl.pallas_call(
        functools.partial(relay_kernel, tile_cells * GROUP),
        out_shape=jax.ShapeDtypeStruct((lax.axis_size(NEAR), C), jnp.float32),
        in_specs=[VMEM],
        out_specs=VMEM,
        name="relay",
        compiler_params=pltpu.CompilerParams(vmem_limit_bytes=4 * MIB),
    )(sums)
    return exchanged(copies, NEAR)


def body(features, gain_one, shift_one, weight_one, bias_one, gain_two, shift_two, weight_two, bias_two):
    frames, rows, width, _ = features.shape
    devices = lax.axis_size(EVERY)
    tile_cells = frames * rows * width
    copies = jax.ShapeDtypeStruct((lax.axis_size(FAR), C), jnp.float32)
    tile = jax.ShapeDtypeStruct(features.shape, jnp.bfloat16)
    two = jax.ShapeDtypeStruct((2, rows, width, C), jnp.bfloat16)
    place = jnp.stack(
        [lax.axis_index("c"), lax.axis_index(TM), lax.axis_index(ROWS), lax.axis_size(ROWS) - 1]
    ).astype(jnp.int32)
    common = dict(
        scratch_shapes=[pltpu.VMEM((frames + 2, rows + 2, width, C), jnp.bfloat16)],
        compiler_params=pltpu.CompilerParams(vmem_limit_bytes=20 * MIB),
    )
    specs = [SMEM] + [VMEM] * 7
    vectors = [v.reshape(1, C) for v in (gain_one, shift_one, bias_one, gain_two, shift_two, bias_two)]

    last, sums, vectors = pl.pallas_call(
        moments_kernel,
        out_shape=(two, copies, jax.ShapeDtypeStruct((8, C), jnp.float32)),
        in_specs=[VMEM] * 7,
        out_specs=(VMEM,) * 3,
        name="moments",
        compiler_params=pltpu.CompilerParams(vmem_limit_bytes=8 * MIB),
    )(features, *vectors)
    around = neighbours(features, last, (-1, 1))
    sums = everywhere(sums, tile_cells)
    hidden, last, sums_two = pl.pallas_call(
        functools.partial(first_conv_kernel, devices),
        out_shape=(tile, two, copies),
        in_specs=specs,
        out_specs=(VMEM,) * 3,
        name="first_conv",
        **common,
    )(place, features, *around, sums, vectors, weight_one)

    around = neighbours(hidden, last, (1, -1))
    sums_two = everywhere(sums_two, tile_cells)
    return pl.pallas_call(
        functools.partial(second_conv_kernel, devices),
        out_shape=tile,
        in_specs=specs + [VMEM],
        out_specs=VMEM,
        name="second_conv",
        **common,
    )(place, hidden, *around, sums_two, vectors, weight_two, features)


def solution(mesh):
    split = Mesh(mesh.devices.reshape(4, 2, 8, 4), EVERY)
    return jax.shard_map(
        body,
        mesh=split,
        in_specs=(P(TM, ROWS, None, None), P(), P(), P(), P(), P(), P(), P(), P()),
        out_specs=P(TM, ROWS, None, None),
        check_vma=False,
    )
```

```python
import functools

import jax
import jax.numpy as jnp
from jax import lax
from jax.experimental import pallas as pl
from jax.experimental.pallas import tpu as pltpu
from jax.sharding import Mesh
from jax.sharding import PartitionSpec as P

C = 128
GROUP = 4
TM = ("y", "c")
ROWS = ("z", "x")
EVERY = TM + ROWS
FAR = ("y", "z")
NEAR = ("c", "x")
EPS = 1e-06
MIB = 1 << 20
VMEM = pl.BlockSpec(memory_space=pltpu.VMEM)
HBM = pl.BlockSpec(memory_space=pltpu.HBM)


def group_total(v):
    lane = lax.broadcasted_iota(jnp.int32, v.shape, v.ndim - 1)
    for step in (1, 2):
        ahead = pltpu.roll(v, C - step, v.ndim - 1)
        behind = pltpu.roll(v, step, v.ndim - 1)
        v = v + jnp.where((lane & step) == 0, ahead, behind)
    return v


def lane_place(shape):
    return lax.broadcasted_iota(jnp.int32, shape, len(shape) - 1) % GROUP


def packed(first, centered):
    place = lane_place(first.shape)
    return jnp.where(place == 0, first, jnp.where(place == 1, centered, 0.0))


def column_total(rows):
    total = jnp.sum(rows.reshape(rows.shape[0] // 8, 8, C), axis=0)
    return jnp.broadcast_to(jnp.sum(total, axis=0, keepdims=True), (8, C))


def merged(every, cells):
    count = every.shape[0]
    total = column_total(every)
    place = lane_place(total.shape)
    first = group_total(jnp.where(place == 0, total, 0.0))
    apart = every / cells - first[:1] / (cells * count)
    between = column_total(apart * apart) * cells
    centered = group_total(jnp.where(place == 0, between, jnp.where(place == 1, total, 0.0)))
    return first, centered


def scale_and_offset(sums_ref, vectors_ref, which, tile_cells, devices):
    count = sums_ref.shape[0]
    cells = tile_cells * GROUP * devices
    first, centered = merged(sums_ref[...], cells // count)
    average, spread = first[:1] / cells, centered[:1] / cells
    scale = lax.rsqrt(spread + EPS) * vectors_ref[which : which + 1]
    offset = vectors_ref[which + 1 : which + 2] - average * scale
    return 0.5 * scale, 0.5 * offset


def activated(values, scale, offset):
    half = values.astype(jnp.float32) * scale + offset
    return (half + half * jnp.tanh(half)).astype(jnp.bfloat16)


def taps(act_ref, w_ref, f, wraps):
    width = act_ref.shape[2]
    column = lax.broadcasted_iota(jnp.int32, (width, C), 0)

    def left(rows, unused):
        pieces = []
        for i in range(3):
            for r in rows:
                piece = act_ref[f + i, r]
                if wraps is not None and r == unused:
                    piece = jnp.where(wraps, jnp.zeros_like(piece), piece)
                pieces.append(piece)
        return jnp.concatenate(pieces, axis=1)

    def block(i, j, k):
        if not 0 <= j < 3:
            return jnp.zeros((C, C), jnp.bfloat16)
        first = ((i * 3 + j) * 3 + k) * C
        return w_ref[first : first + C, :]

    def pair(i, r, out, k):
        found = block(i, r - out, k)
        if wraps is not None and 0 <= r - out < 3 and r // 2 != out:
            found = jnp.where(wraps, jnp.zeros_like(found), found)
        return found

    early = jnp.concatenate(
        [jnp.concatenate([block(i, j, 0), block(i, j, 1)], axis=1) for i in range(3) for j in range(3)],
        axis=0,
    )
    late = jnp.concatenate(
        [jnp.concatenate([pair(i, r, 0, 2), pair(i, r, 1, 2)], axis=1) for i in range(3) for r in range(4)],
        axis=0,
    )
    ends = jnp.dot(left(range(4), None), late, preferred_element_type=jnp.float32)
    totals = []
    for out in range(2):
        part = jnp.dot(left(range(out, out + 3), 2 - out), early, preferred_element_type=jnp.float32)
        before = jnp.where(column == 0, 0.0, pltpu.roll(part[:, :C], 1, 0))
        after = ends[:, out * C : (out + 1) * C]
        after = jnp.where(column == width - 1, 0.0, pltpu.roll(after, width - 1, 0))
        totals.append(before + part[:, C:] + after)
    return totals


def conv(sources, act_ref, w_ref, wraps, emit):
    earlier = 2
    frames, rows = act_ref.shape[0], act_ref.shape[1]

    def fill(f):
        for r in range(rows):
            act_ref[f, r] = sources(f, r)

    for f in range(earlier):
        fill(f)
    for f in range(frames - earlier):
        fill(f + earlier)
        emit(f, taps(act_ref, w_ref, f, wraps))


def source_of(own_ref, rows_ref, back_ref, diagonal_ref, own_low, back_low, tm, scale, offset, hides):
    earlier = back_ref.shape[0]

    def pick(low, one, other, r):
        return jnp.where(low if r < 2 else jnp.logical_not(low), one, other)

    def sources(f, r):
        here = max(f - earlier, 0)
        value = pick(own_low, own_ref[here, r % 2], rows_ref[here, r % 2], r)
        if f < earlier:
            past = pick(back_low, back_ref[f, r % 2], diagonal_ref[f, r % 2], r)
            value = jnp.where(tm == 0, value, past)
        value = activated(value, scale, offset)
        if r in hides:
            value = jnp.where(hides[r], jnp.zeros_like(value), value)
        return value

    return sources


def moments_kernel(x_hbm, *refs):
    vectors_hbm, (last_ref, sums_ref, vectors_ref, x_ref, x_sems, vector_sems) = refs[:-6], refs[-6:]
    frames, rows, width, _ = x_ref.shape
    earlier = last_ref.shape[0]
    copies = [pltpu.make_async_copy(x_hbm.at[f], x_ref.at[f], x_sems.at[f]) for f in range(frames)]
    small = [
        pltpu.make_async_copy(v, vectors_ref.at[i : i + 1], vector_sems.at[i])
        for i, v in enumerate(vectors_hbm)
    ]
    for copy in copies + small:
        copy.start()
    cells = frames * rows * width * GROUP

    def folded(f, step):
        total = jnp.zeros((8, C), jnp.float32)
        for r in range(rows):
            total = total + step(x_ref[f, r].astype(jnp.float32)).reshape(width // 8, 8, C).sum(axis=0)
        return total

    first = jnp.zeros((8, C), jnp.float32)
    for f in range(frames):
        copies[f].wait()
        first = first + folded(f, lambda v: v)
    first = group_total(column_total(first))
    mean = first[:1] / cells
    centered = jnp.zeros((8, C), jnp.float32)
    for f in range(frames):
        centered = centered + folded(f, lambda v: (v - mean) * (v - mean))
    last_ref[...] = x_ref[frames - earlier :]
    both = packed(first, group_total(column_total(centered)))
    sums_ref[...] = jnp.broadcast_to(both[:1], sums_ref.shape)
    for copy in small:
        copy.wait()


def relay_kernel(cells, sums_ref, next_ref):
    both = packed(*merged(sums_ref[...], cells))
    next_ref[...] = jnp.broadcast_to(both[:1], next_ref.shape)


def first_conv_kernel(
    devices, last_row, own_ref, rows_ref, back_ref, diagonal_ref, sums_ref, vectors_ref, w_ref,
    hidden_ref, last_ref, next_ref, act_ref,
):
    frames, rows, width, _ = own_ref.shape
    earlier = back_ref.shape[0]
    core, tm, row = lax.axis_index("c"), lax.axis_index(TM), lax.axis_index(ROWS)
    scale, offset = scale_and_offset(sums_ref, vectors_ref, 0, frames * rows * width, devices)
    low = core == 1
    sources = source_of(own_ref, rows_ref, back_ref, diagonal_ref, low, low, tm, scale, offset, {})
    held = []

    def folded(values):
        return sum(v.reshape(width // 8, 8, C).sum(axis=0) for v in values)

    def emit(f, totals):
        rounded = [(v + vectors_ref[2:3]).astype(jnp.bfloat16) for v in totals]
        for r, v in enumerate(rounded):
            hidden_ref[f, r] = v
            if f >= frames - earlier:
                last_ref[f - frames + earlier, r] = v
        wide = [v.astype(jnp.float32) for v in rounded]
        if not held:
            held.append(jnp.sum(folded(wide), axis=0, keepdims=True) / (rows * width))
        apart = [v - held[0] for v in wide]
        held.append((folded(apart), folded([v * v for v in apart])))

    conv(sources, act_ref, w_ref, row == core * last_row, emit)
    cells = frames * rows * width
    first = jnp.sum(sum(a for a, _ in held[1:]), axis=0, keepdims=True)
    square = jnp.sum(sum(b for _, b in held[1:]), axis=0, keepdims=True)
    mean = held[0] + first / cells
    shape = (8, C)
    whole = group_total(jnp.broadcast_to(mean * cells, shape))
    apart = mean - whole[:1] / (cells * GROUP)
    centered = square - first * first / cells + cells * apart * apart
    both = packed(whole, group_total(jnp.broadcast_to(centered, shape)))
    next_ref[...] = jnp.broadcast_to(both[:1], next_ref.shape)


def second_conv_kernel(
    devices, last_row, own_ref, rows_ref, back_ref, diagonal_ref, sums_ref, vectors_ref, w_ref,
    features_ref, out_ref, act_ref,
):
    frames, rows, width, _ = own_ref.shape
    core, tm, row = lax.axis_index("c"), lax.axis_index(TM), lax.axis_index(ROWS)
    scale, offset = scale_and_offset(sums_ref, vectors_ref, 3, frames * rows * width, devices)
    hides = {0: row == 0, act_ref.shape[1] - 1: row == last_row}
    sources = source_of(
        own_ref, rows_ref, back_ref, diagonal_ref, core == 0, core == 1, tm, scale, offset, hides
    )

    def emit(f, totals):
        for r, v in enumerate(totals):
            value = v + vectors_ref[5:6] + features_ref[f, r].astype(jnp.float32)
            out_ref[f, r] = value.astype(jnp.bfloat16)

    conv(sources, act_ref, w_ref, None, emit)


def sent(block, tm_step, row_steps):
    tms, rows = lax.axis_size(TM), lax.axis_size(ROWS)
    route = []
    for t in range(tms):
        for r in range(rows):
            source = (t - tm_step, (r + row_steps[t % 2]) % rows)
            if source[0] >= 0:
                route.append((source[0] * rows + source[1], t * rows + r))
    return lax.ppermute(block, EVERY, route)


def neighbours(own, last, row_steps):
    beside = sent(own, 0, row_steps)
    back = sent(last, 1, (0, 0))
    diagonal = sent(last, 1, (-1, 1))
    return beside, back, diagonal


def exchanged(copies, axes):
    count = copies.shape[0]
    received = lax.all_to_all(copies.reshape(count, 1, C), axes, split_axis=0, concat_axis=0, tiled=True)
    return received.reshape(count, C)


def everywhere(copies, tile_cells):
    sums = exchanged(copies, FAR)
    copies = pl.pallas_call(
        functools.partial(relay_kernel, tile_cells * GROUP),
        out_shape=jax.ShapeDtypeStruct((lax.axis_size(NEAR), C), jnp.float32),
        in_specs=[VMEM],
        out_specs=VMEM,
        name="relay",
        cost_estimate=pl.CostEstimate(flops=0, bytes_accessed=1 << 24, transcendentals=0),
        compiler_params=pltpu.CompilerParams(vmem_limit_bytes=4 * MIB),
    )(sums)
    return exchanged(copies, NEAR)


def body(features, gain_one, shift_one, weight_one, bias_one, gain_two, shift_two, weight_two, bias_two):
    frames, rows, width, _ = features.shape
    devices = lax.axis_size(EVERY)
    tile_cells = frames * rows * width
    copies = jax.ShapeDtypeStruct((lax.axis_size(FAR), C), jnp.float32)
    tile = jax.ShapeDtypeStruct(features.shape, jnp.bfloat16)
    two = jax.ShapeDtypeStruct((2, rows, width, C), jnp.bfloat16)
    last_row = lax.axis_size(ROWS) - 1
    common = dict(
        scratch_shapes=[pltpu.VMEM((frames + 2, rows + 2, width, C), jnp.bfloat16)],
        compiler_params=pltpu.CompilerParams(vmem_limit_bytes=10 * MIB),
    )
    specs = [VMEM] * 7
    vectors = [v.reshape(1, C) for v in (gain_one, shift_one, bias_one, gain_two, shift_two, bias_two)]

    last, sums, vectors = pl.pallas_call(
        moments_kernel,
        out_shape=(two, copies, jax.ShapeDtypeStruct((8, C), jnp.float32)),
        in_specs=[HBM] * 7,
        out_specs=(VMEM,) * 3,
        scratch_shapes=[
            pltpu.VMEM(features.shape, jnp.bfloat16),
            pltpu.SemaphoreType.DMA((frames,)),
            pltpu.SemaphoreType.DMA((len(vectors),)),
        ],
        name="moments",
        compiler_params=pltpu.CompilerParams(vmem_limit_bytes=4 * MIB),
    )(features, *vectors)
    around = neighbours(features, last, (-1, 1))
    sums = everywhere(sums, tile_cells)
    hidden, last, sums_two = pl.pallas_call(
        functools.partial(first_conv_kernel, devices, last_row),
        out_shape=(tile, two, copies),
        in_specs=specs,
        out_specs=(VMEM,) * 3,
        name="first_conv",
        **common,
    )(features, *around, sums, vectors, weight_one)

    around = neighbours(hidden, last, (1, -1))
    sums_two = everywhere(sums_two, tile_cells)
    return pl.pallas_call(
        functools.partial(second_conv_kernel, devices, last_row),
        out_shape=tile,
        in_specs=specs + [VMEM],
        out_specs=VMEM,
        name="second_conv",
        **common,
    )(hidden, *around, sums_two, vectors, weight_two, features)


def solution(mesh):
    split = Mesh(mesh.devices.reshape(4, 2, 8, 4), EVERY)
    return jax.shard_map(
        body,
        mesh=split,
        in_specs=(P(TM, ROWS, None, None), P(), P(), P(), P(), P(), P(), P(), P()),
        out_specs=P(TM, ROWS, None, None),
        check_vma=False,
    )
```

```python
import functools

import jax
import jax.numpy as jnp
from jax import lax
from jax.experimental import pallas as pl
from jax.experimental.pallas import tpu as pltpu
from jax.sharding import Mesh
from jax.sharding import PartitionSpec as P

C = 128
GROUP = 4
TM = ("y", "c")
ROWS = ("z", "x")
EVERY = TM + ROWS
STAGES_ONE = (("y", "c", "z"), ("x",))
STAGES_TWO = (("y", "z"), ("c", "x"))
EPS = 1e-06
MIB = 1 << 20
VMEM = pl.BlockSpec(memory_space=pltpu.VMEM)
HBM = pl.BlockSpec(memory_space=pltpu.HBM)


def group_total(v):
    lane = lax.broadcasted_iota(jnp.int32, v.shape, v.ndim - 1)
    for step in (1, 2):
        ahead = pltpu.roll(v, C - step, v.ndim - 1)
        behind = pltpu.roll(v, step, v.ndim - 1)
        v = v + jnp.where((lane & step) == 0, ahead, behind)
    return v


def lane_place(shape):
    return lax.broadcasted_iota(jnp.int32, shape, len(shape) - 1) % GROUP


def packed(first, centered):
    place = lane_place(first.shape)
    return jnp.where(place == 0, first, jnp.where(place == 1, centered, 0.0))


def column_total(rows):
    total = rows if rows.shape[0] < 8 else jnp.sum(rows.reshape(rows.shape[0] // 8, 8, C), axis=0)
    return jnp.broadcast_to(jnp.sum(total, axis=0, keepdims=True), (8, C))


def merged(every, cells):
    count = every.shape[0]
    total = column_total(every)
    place = lane_place(total.shape)
    first = group_total(jnp.where(place == 0, total, 0.0))
    apart = every / cells - first[:1] / (cells * count)
    between = column_total(apart * apart) * cells
    centered = group_total(jnp.where(place == 0, between, jnp.where(place == 1, total, 0.0)))
    return first, centered


def scale_and_offset(sums_ref, vectors_ref, which, tile_cells, devices):
    count = sums_ref.shape[0]
    cells = tile_cells * GROUP * devices
    first, centered = merged(sums_ref[...], cells // count)
    average, spread = first[:1] / cells, centered[:1] / cells
    scale = lax.rsqrt(spread + EPS) * vectors_ref[which : which + 1]
    offset = vectors_ref[which + 1 : which + 2] - average * scale
    return 0.5 * scale, 0.5 * offset


def activated(values, scale, offset):
    half = values.astype(jnp.float32) * scale + offset
    return (half + half * jnp.tanh(half)).astype(jnp.bfloat16)


def taps(act_ref, w_ref, f, wraps):
    width = act_ref.shape[2]
    column = lax.broadcasted_iota(jnp.int32, (width, C), 0)

    def left(rows, unused):
        pieces = []
        for i in range(3):
            for r in rows:
                piece = act_ref[f + i, r]
                if wraps is not None and r == unused:
                    piece = jnp.where(wraps, jnp.zeros_like(piece), piece)
                pieces.append(piece)
        return jnp.concatenate(pieces, axis=1)

    def block(i, j, k):
        if not 0 <= j < 3:
            return jnp.zeros((C, C), jnp.bfloat16)
        first = ((i * 3 + j) * 3 + k) * C
        return w_ref[first : first + C, :]

    def pair(i, r, out, k):
        found = block(i, r - out, k)
        if wraps is not None and 0 <= r - out < 3 and r // 2 != out:
            found = jnp.where(wraps, jnp.zeros_like(found), found)
        return found

    early = jnp.concatenate(
        [jnp.concatenate([block(i, j, 0), block(i, j, 1)], axis=1) for i in range(3) for j in range(3)],
        axis=0,
    )
    late = jnp.concatenate(
        [jnp.concatenate([pair(i, r, 0, 2), pair(i, r, 1, 2)], axis=1) for i in range(3) for r in range(4)],
        axis=0,
    )
    ends = jnp.dot(left(range(4), None), late, preferred_element_type=jnp.float32)
    totals = []
    for out in range(2):
        part = jnp.dot(left(range(out, out + 3), 2 - out), early, preferred_element_type=jnp.float32)
        before = jnp.where(column == 0, 0.0, pltpu.roll(part[:, :C], 1, 0))
        after = ends[:, out * C : (out + 1) * C]
        after = jnp.where(column == width - 1, 0.0, pltpu.roll(after, width - 1, 0))
        totals.append(before + part[:, C:] + after)
    return totals


def conv(sources, act_ref, w_ref, wraps, emit, ready=None):
    earlier = 2
    frames, rows = act_ref.shape[0], act_ref.shape[1]

    def fill(f):
        for r in range(rows):
            act_ref[f, r] = sources(f, r)

    for f in range(earlier + 2):
        fill(f)
    if ready is not None:
        ready()
    for f in range(frames - earlier):
        if f > 1:
            fill(f + earlier)
        emit(f, taps(act_ref, w_ref, f, wraps))


def source_of(own_ref, rows_ref, back_ref, diagonal_ref, own_low, back_low, tm, scale, offset, hides):
    earlier = back_ref.shape[0]

    def pick(low, one, other, r):
        return jnp.where(low if r < 2 else jnp.logical_not(low), one, other)

    def sources(f, r):
        here = max(f - earlier, 0)
        value = pick(own_low, own_ref[here, r % 2], rows_ref[here, r % 2], r)
        if f < earlier:
            past = pick(back_low, back_ref[f, r % 2], diagonal_ref[f, r % 2], r)
            value = jnp.where(tm == 0, value, past)
        value = activated(value, scale, offset)
        if r in hides:
            value = jnp.where(hides[r], jnp.zeros_like(value), value)
        return value

    return sources


class Sums:
    def __init__(self, rows, width):
        self.cells, self.width = rows * width, width
        self.center, self.firsts, self.squares = None, [], []

    def folded(self, values):
        return sum(v.reshape(self.width // 8, 8, C).sum(axis=0) for v in values)

    def add(self, values):
        if self.center is None:
            self.center = jnp.sum(self.folded(values), axis=0, keepdims=True) / self.cells
        apart = [v - self.center for v in values]
        self.firsts.append(self.folded(apart))
        self.squares.append(self.folded([v * v for v in apart]))

    def both(self):
        cells = self.cells * len(self.firsts)
        first = jnp.sum(sum(self.firsts), axis=0, keepdims=True)
        square = jnp.sum(sum(self.squares), axis=0, keepdims=True)
        mean = self.center + first / cells
        whole = group_total(jnp.broadcast_to(mean * cells, (8, C)))
        apart = mean - whole[:1] / (cells * GROUP)
        centered = square - first * first / cells + cells * apart * apart
        return packed(whole, group_total(jnp.broadcast_to(centered, (8, C))))


def moments_kernel(x_hbm, *refs):
    vectors_hbm, (last_ref, sums_ref, vectors_ref, x_ref, x_sems, vector_sems) = refs[:-6], refs[-6:]
    frames, rows, width, _ = x_ref.shape
    earlier = last_ref.shape[0]
    copies = [pltpu.make_async_copy(x_hbm.at[f], x_ref.at[f], x_sems.at[f]) for f in range(frames)]
    small = [
        pltpu.make_async_copy(v, vectors_ref.at[i : i + 1], vector_sems.at[i])
        for i, v in enumerate(vectors_hbm)
    ]
    for copy in copies + small:
        copy.start()
    sums = Sums(rows, width)
    for f in range(frames):
        copies[f].wait()
        sums.add([x_ref[f, r].astype(jnp.float32) for r in range(rows)])
        if f >= frames - earlier:
            last_ref[f - frames + earlier] = x_ref[f]
    sums_ref[...] = jnp.broadcast_to(sums.both()[:1], sums_ref.shape)
    for copy in small:
        copy.wait()


def relay_kernel(cells, sums_ref, next_ref):
    both = packed(*merged(sums_ref[...], cells))
    next_ref[...] = jnp.broadcast_to(both[:1], next_ref.shape)


def first_conv_kernel(
    devices, last_row, own_ref, rows_ref, back_ref, diagonal_ref, sums_ref, vectors_ref, w_hbm,
    hidden_ref, last_ref, next_ref, act_ref, w_ref, w_sem,
):
    weights = pltpu.make_async_copy(w_hbm, w_ref, w_sem)
    weights.start()
    frames, rows, width, _ = own_ref.shape
    earlier = back_ref.shape[0]
    core, tm, row = lax.axis_index("c"), lax.axis_index(TM), lax.axis_index(ROWS)
    scale, offset = scale_and_offset(sums_ref, vectors_ref, 0, frames * rows * width, devices)
    low = core == 1
    sources = source_of(own_ref, rows_ref, back_ref, diagonal_ref, low, low, tm, scale, offset, {})
    sums = Sums(rows, width)

    def emit(f, totals):
        rounded = [(v + vectors_ref[2:3]).astype(jnp.bfloat16) for v in totals]
        for r, v in enumerate(rounded):
            hidden_ref[f, r] = v
            if f >= frames - earlier:
                last_ref[f - frames + earlier, r] = v
        sums.add([v.astype(jnp.float32) for v in rounded])

    conv(sources, act_ref, w_ref, row == core * last_row, emit, weights.wait)
    next_ref[...] = jnp.broadcast_to(sums.both()[:1], next_ref.shape)


def second_conv_kernel(
    devices, last_row, own_ref, rows_ref, back_ref, diagonal_ref, sums_ref, vectors_ref, w_hbm,
    features_hbm, out_hbm, act_ref, w_ref, w_sem, features_ref, sem, out_ref, out_sems,
):
    weights = pltpu.make_async_copy(w_hbm, w_ref, w_sem)
    weights.start()
    residual = pltpu.make_async_copy(features_hbm, features_ref, sem)
    residual.start()
    frames, rows, width, _ = own_ref.shape
    core, tm, row = lax.axis_index("c"), lax.axis_index(TM), lax.axis_index(ROWS)
    scale, offset = scale_and_offset(sums_ref, vectors_ref, 3, frames * rows * width, devices)
    hides = {0: row == 0, act_ref.shape[1] - 1: row == last_row}
    sources = source_of(
        own_ref, rows_ref, back_ref, diagonal_ref, core == 0, core == 1, tm, scale, offset, hides
    )

    def emit(f, totals):
        for r, v in enumerate(totals):
            value = v + vectors_ref[5:6] + features_ref[f, r].astype(jnp.float32)
            out_ref[f, r] = value.astype(jnp.bfloat16)
        outs[f].start()

    outs = [pltpu.make_async_copy(out_ref.at[f], out_hbm.at[f], out_sems.at[f]) for f in range(frames)]

    def ready():
        weights.wait()
        residual.wait()

    conv(sources, act_ref, w_ref, None, emit, ready)
    for copy in outs:
        copy.wait()


def sent(block, tm_step, row_steps):
    tms, rows = lax.axis_size(TM), lax.axis_size(ROWS)
    route = []
    for t in range(tms):
        for r in range(rows):
            source = (t - tm_step, (r + row_steps[t % 2]) % rows)
            if source[0] >= 0:
                route.append((source[0] * rows + source[1], t * rows + r))
    return lax.ppermute(block, EVERY, route)


def neighbours(own, last, row_steps):
    beside = sent(own, 0, row_steps)
    back = sent(last, 1, (0, 0))
    diagonal = sent(last, 1, (-1, 1))
    return beside, back, diagonal


def in_hbm(array):
    return pltpu.with_memory_space_constraint(array, pltpu.HBM)


def exchanged(copies, axes):
    count = copies.shape[0]
    received = lax.all_to_all(copies.reshape(count, 1, C), axes, split_axis=0, concat_axis=0, tiled=True)
    return received.reshape(count, C)


def everywhere(copies, tile_cells, stages):
    far, near = stages
    sums = exchanged(copies, far)
    copies = pl.pallas_call(
        functools.partial(relay_kernel, tile_cells * GROUP),
        out_shape=jax.ShapeDtypeStruct((lax.axis_size(near), C), jnp.float32),
        in_specs=[VMEM],
        out_specs=VMEM,
        name="relay",
        cost_estimate=pl.CostEstimate(flops=0, bytes_accessed=1 << 24, transcendentals=0),
        compiler_params=pltpu.CompilerParams(vmem_limit_bytes=4 * MIB),
    )(sums)
    return exchanged(copies, near)


def body(features, gain_one, shift_one, weight_one, bias_one, gain_two, shift_two, weight_two, bias_two):
    frames, rows, width, _ = features.shape
    devices = lax.axis_size(EVERY)
    tile_cells = frames * rows * width
    copies_one, copies_two = (
        jax.ShapeDtypeStruct((lax.axis_size(stages[0]), C), jnp.float32) for stages in (STAGES_ONE, STAGES_TWO)
    )
    tile = jax.ShapeDtypeStruct(features.shape, jnp.bfloat16)
    two = jax.ShapeDtypeStruct((2, rows, width, C), jnp.bfloat16)
    last_row = lax.axis_size(ROWS) - 1
    held = pltpu.VMEM((frames + 2, rows + 2, width, C), jnp.bfloat16)
    limit = pltpu.CompilerParams(vmem_limit_bytes=10 * MIB)
    vectors = [v.reshape(1, C) for v in (gain_one, shift_one, bias_one, gain_two, shift_two, bias_two)]

    last, sums, vectors = pl.pallas_call(
        moments_kernel,
        out_shape=(two, copies_one, jax.ShapeDtypeStruct((8, C), jnp.float32)),
        in_specs=[HBM] * 7,
        out_specs=(VMEM,) * 3,
        scratch_shapes=[
            pltpu.VMEM(features.shape, jnp.bfloat16),
            pltpu.SemaphoreType.DMA((frames,)),
            pltpu.SemaphoreType.DMA((len(vectors),)),
        ],
        name="moments",
        compiler_params=pltpu.CompilerParams(vmem_limit_bytes=4 * MIB),
    )(*(in_hbm(v) for v in (features, *vectors)))
    around = neighbours(features, last, (-1, 1))
    sums = everywhere(sums, tile_cells, STAGES_ONE)
    hidden, last, sums_two = pl.pallas_call(
        functools.partial(first_conv_kernel, devices, last_row),
        out_shape=(tile, two, copies_two),
        in_specs=[VMEM] * 6 + [HBM],
        out_specs=(VMEM,) * 3,
        scratch_shapes=[held, pltpu.VMEM(weight_one.shape, weight_one.dtype), pltpu.SemaphoreType.DMA],
        name="first_conv",
        compiler_params=limit,
    )(features, *around, sums, vectors, in_hbm(weight_one))

    around = neighbours(hidden, last, (1, -1))
    sums_two = everywhere(sums_two, tile_cells, STAGES_TWO)
    return pl.pallas_call(
        functools.partial(second_conv_kernel, devices, last_row),
        out_shape=tile,
        in_specs=[VMEM] * 6 + [HBM] * 2,
        out_specs=HBM,
        scratch_shapes=[
            held,
            pltpu.VMEM(weight_two.shape, weight_two.dtype),
            pltpu.SemaphoreType.DMA,
            pltpu.VMEM(features.shape, features.dtype),
            pltpu.SemaphoreType.DMA,
            pltpu.VMEM(features.shape, features.dtype),
            pltpu.SemaphoreType.DMA((frames,)),
        ],
        name="second_conv",
        compiler_params=limit,
    )(hidden, *around, sums_two, vectors, in_hbm(weight_two), in_hbm(features))


def solution(mesh):
    split = Mesh(mesh.devices.reshape(4, 2, 8, 4), EVERY)
    return jax.shard_map(
        body,
        mesh=split,
        in_specs=(P(TM, ROWS, None, None), P(), P(), P(), P(), P(), P(), P(), P()),
        out_specs=P(TM, ROWS, None, None),
        check_vma=False,
    )
```

```python
import functools

import jax
import jax.numpy as jnp
from jax import lax
from jax.experimental import pallas as pl
from jax.experimental.pallas import tpu as pltpu
from jax.sharding import Mesh
from jax.sharding import PartitionSpec as P

C = 128
GROUP = 4
TM = ("y", "c")
ROWS = ("z", "x")
EVERY = TM + ROWS
FAR = ("y", "z")
NEAR = ("c", "x")
EPS = 1e-06
MIB = 1 << 20
VMEM = pl.BlockSpec(memory_space=pltpu.VMEM)
HBM = pl.BlockSpec(memory_space=pltpu.HBM)


def group_total(v):
    lane = lax.broadcasted_iota(jnp.int32, v.shape, v.ndim - 1)
    for step in (1, 2):
        ahead = pltpu.roll(v, C - step, v.ndim - 1)
        behind = pltpu.roll(v, step, v.ndim - 1)
        v = v + jnp.where((lane & step) == 0, ahead, behind)
    return v


def lane_place(shape):
    return lax.broadcasted_iota(jnp.int32, shape, len(shape) - 1) % GROUP


def packed(first, centered):
    place = lane_place(first.shape)
    return jnp.where(place == 0, first, jnp.where(place == 1, centered, 0.0))


def column_total(rows):
    total = jnp.sum(rows.reshape(rows.shape[0] // 8, 8, C), axis=0)
    return jnp.broadcast_to(jnp.sum(total, axis=0, keepdims=True), (8, C))


def merged(every, cells):
    count = every.shape[0]
    total = column_total(every)
    place = lane_place(total.shape)
    first = group_total(jnp.where(place == 0, total, 0.0))
    apart = every / cells - first[:1] / (cells * count)
    between = column_total(apart * apart) * cells
    centered = group_total(jnp.where(place == 0, between, jnp.where(place == 1, total, 0.0)))
    return first, centered


def scale_and_offset(sums_ref, vectors_ref, which, tile_cells, devices):
    count = sums_ref.shape[0]
    cells = tile_cells * GROUP * devices
    first, centered = merged(sums_ref[...], cells // count)
    average, spread = first[:1] / cells, centered[:1] / cells
    scale = lax.rsqrt(spread + EPS) * vectors_ref[which : which + 1]
    offset = vectors_ref[which + 1 : which + 2] - average * scale
    return 0.5 * scale, 0.5 * offset


def activated(values, scale, offset):
    half = values.astype(jnp.float32) * scale + offset
    return (half + half * jnp.tanh(half)).astype(jnp.bfloat16)


def taps(act_ref, w_ref, f, wraps):
    width = act_ref.shape[2]
    column = lax.broadcasted_iota(jnp.int32, (width, C), 0)

    def left(rows, unused):
        pieces = []
        for i in range(3):
            for r in rows:
                piece = act_ref[f + i, r]
                if wraps is not None and r == unused:
                    piece = jnp.where(wraps, jnp.zeros_like(piece), piece)
                pieces.append(piece)
        return jnp.concatenate(pieces, axis=1)

    def block(i, j, k):
        if not 0 <= j < 3:
            return jnp.zeros((C, C), jnp.bfloat16)
        first = ((i * 3 + j) * 3 + k) * C
        return w_ref[first : first + C, :]

    def pair(i, r, out, k):
        found = block(i, r - out, k)
        if wraps is not None and 0 <= r - out < 3 and r // 2 != out:
            found = jnp.where(wraps, jnp.zeros_like(found), found)
        return found

    early = jnp.concatenate(
        [jnp.concatenate([block(i, j, 0), block(i, j, 1)], axis=1) for i in range(3) for j in range(3)],
        axis=0,
    )
    late = jnp.concatenate(
        [jnp.concatenate([pair(i, r, 0, 2), pair(i, r, 1, 2)], axis=1) for i in range(3) for r in range(4)],
        axis=0,
    )
    ends = jnp.dot(left(range(4), None), late, preferred_element_type=jnp.float32)
    totals = []
    for out in range(2):
        part = jnp.dot(left(range(out, out + 3), 2 - out), early, preferred_element_type=jnp.float32)
        before = jnp.where(column == 0, 0.0, pltpu.roll(part[:, :C], 1, 0))
        after = ends[:, out * C : (out + 1) * C]
        after = jnp.where(column == width - 1, 0.0, pltpu.roll(after, width - 1, 0))
        totals.append(before + part[:, C:] + after)
    return totals


def conv(sources, act_ref, w_ref, wraps, emit, ready=None):
    earlier = 2
    frames, rows = act_ref.shape[0], act_ref.shape[1]

    def fill(f):
        for r in range(rows):
            act_ref[f, r] = sources(f, r)

    for f in range(earlier + 2):
        fill(f)
    if ready is not None:
        ready()
    for f in range(frames - earlier):
        if f > 1:
            fill(f + earlier)
        emit(f, taps(act_ref, w_ref, f, wraps))


def source_of(own_ref, rows_ref, back_ref, diagonal_ref, own_low, back_low, tm, scale, offset, hides):
    earlier = back_ref.shape[0]

    def pick(low, one, other, r):
        return jnp.where(low if r < 2 else jnp.logical_not(low), one, other)

    def sources(f, r):
        here = max(f - earlier, 0)
        value = pick(own_low, own_ref[here, r % 2], rows_ref[here, r % 2], r)
        if f < earlier:
            past = pick(back_low, back_ref[f, r % 2], diagonal_ref[f, r % 2], r)
            value = jnp.where(tm == 0, value, past)
        value = activated(value, scale, offset)
        if r in hides:
            value = jnp.where(hides[r], jnp.zeros_like(value), value)
        return value

    return sources


class Sums:
    def __init__(self, rows, width):
        self.cells, self.width = rows * width, width
        self.center, self.firsts, self.squares = None, [], []

    def folded(self, values):
        return sum(v.reshape(self.width // 8, 8, C).sum(axis=0) for v in values)

    def add(self, values):
        if self.center is None:
            self.center = jnp.sum(self.folded(values), axis=0, keepdims=True) / self.cells
        apart = [v - self.center for v in values]
        self.firsts.append(self.folded(apart))
        self.squares.append(self.folded([v * v for v in apart]))

    def both(self):
        cells = self.cells * len(self.firsts)
        first = jnp.sum(sum(self.firsts), axis=0, keepdims=True)
        square = jnp.sum(sum(self.squares), axis=0, keepdims=True)
        mean = self.center + first / cells
        whole = group_total(jnp.broadcast_to(mean * cells, (8, C)))
        apart = mean - whole[:1] / (cells * GROUP)
        centered = square - first * first / cells + cells * apart * apart
        return packed(whole, group_total(jnp.broadcast_to(centered, (8, C))))


def moments_kernel(x_hbm, *refs):
    vectors_hbm, (last_ref, sums_ref, vectors_ref, x_ref, x_sems, vector_sems) = refs[:-6], refs[-6:]
    frames, rows, width, _ = x_ref.shape
    earlier = last_ref.shape[0]
    copies = [pltpu.make_async_copy(x_hbm.at[f], x_ref.at[f], x_sems.at[f]) for f in range(frames)]
    small = [
        pltpu.make_async_copy(v, vectors_ref.at[i : i + 1], vector_sems.at[i])
        for i, v in enumerate(vectors_hbm)
    ]
    for copy in copies + small:
        copy.start()
    sums = Sums(rows, width)
    for f in range(frames):
        copies[f].wait()
        sums.add([x_ref[f, r].astype(jnp.float32) for r in range(rows)])
        if f >= frames - earlier:
            last_ref[f - frames + earlier] = x_ref[f]
    sums_ref[...] = jnp.broadcast_to(sums.both()[:1], sums_ref.shape)
    for copy in small:
        copy.wait()


def relay_kernel(cells, sums_ref, next_ref):
    both = packed(*merged(sums_ref[...], cells))
    next_ref[...] = jnp.broadcast_to(both[:1], next_ref.shape)


def first_conv_kernel(
    devices, last_row, own_ref, rows_ref, back_ref, diagonal_ref, sums_ref, vectors_ref, w_hbm,
    hidden_ref, last_ref, next_ref, act_ref, w_ref, w_sem,
):
    weights = pltpu.make_async_copy(w_hbm, w_ref, w_sem)
    weights.start()
    frames, rows, width, _ = own_ref.shape
    earlier = back_ref.shape[0]
    core, tm, row = lax.axis_index("c"), lax.axis_index(TM), lax.axis_index(ROWS)
    scale, offset = scale_and_offset(sums_ref, vectors_ref, 0, frames * rows * width, devices)
    low = core == 1
    sources = source_of(own_ref, rows_ref, back_ref, diagonal_ref, low, low, tm, scale, offset, {})
    sums = Sums(rows, width)

    def emit(f, totals):
        rounded = [(v + vectors_ref[2:3]).astype(jnp.bfloat16) for v in totals]
        for r, v in enumerate(rounded):
            hidden_ref[f, r] = v
            if f >= frames - earlier:
                last_ref[f - frames + earlier, r] = v
        sums.add([v.astype(jnp.float32) for v in rounded])

    conv(sources, act_ref, w_ref, row == core * last_row, emit, weights.wait)
    next_ref[...] = jnp.broadcast_to(sums.both()[:1], next_ref.shape)


def second_conv_kernel(
    devices, last_row, own_ref, rows_ref, back_ref, diagonal_ref, sums_ref, vectors_ref, w_hbm,
    features_hbm, out_hbm, act_ref, w_ref, w_sem, features_ref, sem, out_ref, out_sems,
):
    weights = pltpu.make_async_copy(w_hbm, w_ref, w_sem)
    weights.start()
    residual = pltpu.make_async_copy(features_hbm, features_ref, sem)
    residual.start()
    frames, rows, width, _ = own_ref.shape
    core, tm, row = lax.axis_index("c"), lax.axis_index(TM), lax.axis_index(ROWS)
    scale, offset = scale_and_offset(sums_ref, vectors_ref, 3, frames * rows * width, devices)
    hides = {0: row == 0, act_ref.shape[1] - 1: row == last_row}
    sources = source_of(
        own_ref, rows_ref, back_ref, diagonal_ref, core == 0, core == 1, tm, scale, offset, hides
    )

    def emit(f, totals):
        for r, v in enumerate(totals):
            value = v + vectors_ref[5:6] + features_ref[f, r].astype(jnp.float32)
            out_ref[f, r] = value.astype(jnp.bfloat16)
        outs[f].start()

    outs = [pltpu.make_async_copy(out_ref.at[f], out_hbm.at[f], out_sems.at[f]) for f in range(frames)]

    def ready():
        weights.wait()
        residual.wait()

    conv(sources, act_ref, w_ref, None, emit, ready)
    for copy in outs:
        copy.wait()


def sent(block, tm_step, row_steps):
    tms, rows = lax.axis_size(TM), lax.axis_size(ROWS)
    route = []
    for t in range(tms):
        for r in range(rows):
            source = (t - tm_step, (r + row_steps[t % 2]) % rows)
            if source[0] >= 0:
                route.append((source[0] * rows + source[1], t * rows + r))
    return lax.ppermute(block, EVERY, route)


def neighbours(own, last, row_steps):
    beside = sent(own, 0, row_steps)
    back = sent(last, 1, (0, 0))
    diagonal = sent(last, 1, (-1, 1))
    return beside, back, diagonal


def in_hbm(array):
    return pltpu.with_memory_space_constraint(array, pltpu.HBM)


def exchanged(copies, axes):
    count = copies.shape[0]
    received = lax.all_to_all(copies.reshape(count, 1, C), axes, split_axis=0, concat_axis=0, tiled=True)
    return received.reshape(count, C)


def everywhere(copies, tile_cells):
    sums = exchanged(copies, FAR)
    copies = pl.pallas_call(
        functools.partial(relay_kernel, tile_cells * GROUP),
        out_shape=jax.ShapeDtypeStruct((lax.axis_size(NEAR), C), jnp.float32),
        in_specs=[VMEM],
        out_specs=VMEM,
        name="relay",
        cost_estimate=pl.CostEstimate(flops=0, bytes_accessed=1 << 24, transcendentals=0),
        compiler_params=pltpu.CompilerParams(vmem_limit_bytes=4 * MIB),
    )(sums)
    return exchanged(copies, NEAR)


def body(features, gain_one, shift_one, weight_one, bias_one, gain_two, shift_two, weight_two, bias_two):
    frames, rows, width, _ = features.shape
    devices = lax.axis_size(EVERY)
    tile_cells = frames * rows * width
    copies = jax.ShapeDtypeStruct((lax.axis_size(FAR), C), jnp.float32)
    tile = jax.ShapeDtypeStruct(features.shape, jnp.bfloat16)
    two = jax.ShapeDtypeStruct((2, rows, width, C), jnp.bfloat16)
    last_row = lax.axis_size(ROWS) - 1
    held = pltpu.VMEM((frames + 2, rows + 2, width, C), jnp.bfloat16)
    limit = pltpu.CompilerParams(vmem_limit_bytes=10 * MIB)
    vectors = [v.reshape(1, C) for v in (gain_one, shift_one, bias_one, gain_two, shift_two, bias_two)]

    last, sums, vectors = pl.pallas_call(
        moments_kernel,
        out_shape=(two, copies, jax.ShapeDtypeStruct((8, C), jnp.float32)),
        in_specs=[HBM] * 7,
        out_specs=(VMEM,) * 3,
        scratch_shapes=[
            pltpu.VMEM(features.shape, jnp.bfloat16),
            pltpu.SemaphoreType.DMA((frames,)),
            pltpu.SemaphoreType.DMA((len(vectors),)),
        ],
        name="moments",
        compiler_params=pltpu.CompilerParams(vmem_limit_bytes=4 * MIB),
    )(*(in_hbm(v) for v in (features, *vectors)))
    around = neighbours(features, last, (-1, 1))
    sums = everywhere(sums, tile_cells)
    hidden, last, sums_two = pl.pallas_call(
        functools.partial(first_conv_kernel, devices, last_row),
        out_shape=(tile, two, copies),
        in_specs=[VMEM] * 6 + [HBM],
        out_specs=(VMEM,) * 3,
        scratch_shapes=[held, pltpu.VMEM(weight_one.shape, weight_one.dtype), pltpu.SemaphoreType.DMA],
        name="first_conv",
        compiler_params=limit,
    )(features, *around, sums, vectors, in_hbm(weight_one))

    around = neighbours(hidden, last, (1, -1))
    sums_two = everywhere(sums_two, tile_cells)
    return pl.pallas_call(
        functools.partial(second_conv_kernel, devices, last_row),
        out_shape=tile,
        in_specs=[VMEM] * 6 + [HBM] * 2,
        out_specs=HBM,
        scratch_shapes=[
            held,
            pltpu.VMEM(weight_two.shape, weight_two.dtype),
            pltpu.SemaphoreType.DMA,
            pltpu.VMEM(features.shape, features.dtype),
            pltpu.SemaphoreType.DMA,
            pltpu.VMEM(features.shape, features.dtype),
            pltpu.SemaphoreType.DMA((frames,)),
        ],
        name="second_conv",
        compiler_params=limit,
    )(hidden, *around, sums_two, vectors, in_hbm(weight_two), in_hbm(features))


def solution(mesh):
    split = Mesh(mesh.devices.reshape(4, 2, 8, 4), EVERY)
    return jax.shard_map(
        body,
        mesh=split,
        in_specs=(P(TM, ROWS, None, None), P(), P(), P(), P(), P(), P(), P(), P()),
        out_specs=P(TM, ROWS, None, None),
        check_vma=False,
    )
```
